32 devices in a mesh: outer: 4 (over y, core), inner: 8 (over z, x).
Axes of the slice: x: 2, y: 2, z: 4, core: 2. Of those that a mesh axis runs over, the one named last changes fastest.
Arguments:
- queries: bfloat16 [8192, 4096], P(('outer', 'inner')), may hold values from -120 to 120
- keys_values: bfloat16 [8192, 2, 1024], P(('outer', 'inner')), may hold values from -6.1 to 6.1
- random_blocks: int32 [64, 3], replicated, may hold values from 0 to 63, as said below
- global_blocks: int32 [2], replicated, may hold values from 0 to 63, as said below
Outputs:
- attended: bfloat16 [8192, 4096], P(('outer', 'inner'))
The draws below stay inside these ranges and needn't reach their ends.
Inputs may be any that keep to these rules, and one draw needn't show every extreme that they name: `random_blocks`: among the 48 entries of the rows k * 16 to (k + 1) * 16 - 1, those naming blocks of one range s * 16 to (s + 1) * 16 - 1 number at most 15; for each k exactly 15 name one such range, chosen by the seed. `global_blocks`: the 2 ids are distinct.
All inputs are finite; a program needn't handle non-finite values.
Results may differ from the reference program's by a relative error of at most 0.0046.
Values may be sent and summed in bfloat16 or wider, within the bound.
A program may use at most 128 MiB of HBM per device.

```python
import jax
import jax.numpy as jnp
from jax import lax

HQ = 32
KVH = 8
HD = 128
BLOCK = 128
WIN = 1
GLOB = 2
RAND = 3
SHARDS = 4
BLK_SHARD = 16
NBLK = 64
SEQ = 8192
CAP = 15
KB = 8


def draw_pair(key):
    splits = jax.random.split(key, 3)
    query_part = jnp.clip(jax.random.normal(splits[0], (SEQ, HQ, HD)), -6.0, 6.0)
    key_part = jnp.clip(jax.random.normal(splits[1], (SEQ, KVH, HD)), -6.0, 6.0)
    value_part = jnp.clip(jax.random.normal(splits[2], (SEQ, KVH, HD)), -6.0, 6.0)
    return (query_part, key_part, value_part)


def draw_queries(key, part):
    query_part, key_part, value_part = draw_pair(jax.random.fold_in(key, 11))
    return query_part.reshape(SEQ, HQ * HD).astype(jnp.bfloat16)


def draw_keys_values(key, part):
    query_part, key_part, value_part = draw_pair(jax.random.fold_in(key, 11))
    stacked = jnp.stack([key_part, value_part], axis=1)
    return stacked.reshape(SEQ, 2, KVH * HD).astype(jnp.bfloat16)


def draw_random_blocks(key, part):
    splits = jax.random.split(jax.random.fold_in(key, 23), 3)
    slot_count = BLK_SHARD * RAND
    heavy = jax.random.randint(splits[0], (SHARDS,), 0, SHARDS)
    slot_ids = jnp.arange(slot_count, dtype=jnp.int32)
    others = (slot_ids - CAP) % (SHARDS - 1)
    others = others[None, :] + (others[None, :] >= heavy[:, None]).astype(jnp.int32)
    owners = jnp.where(slot_ids[None, :] < CAP, heavy[:, None], others)
    orders = jax.vmap(lambda single: jax.random.permutation(single, slot_count))(jax.random.split(splits[1], SHARDS))
    owners = jnp.take_along_axis(owners, orders, axis=1)
    within = jax.random.randint(splits[2], (SHARDS, slot_count), 0, BLK_SHARD)
    return (owners * BLK_SHARD + within).reshape(NBLK, RAND).astype(jnp.int32)


def draw_global_blocks(key, part):
    return jax.random.permutation(jax.random.fold_in(key, 31), NBLK)[:GLOB].astype(jnp.int32)


def setup_inputs(seed: int = 0) -> dict:
    key_of = jax.random.split(jax.random.key(seed), 5)
    queries = draw_queries(jax.random.fold_in(key_of[4], 71), 0)
    keys_values = draw_keys_values(jax.random.fold_in(key_of[4], 71), 0)
    random_blocks = draw_random_blocks(jax.random.fold_in(key_of[4], 71), 0)
    global_blocks = draw_global_blocks(jax.random.fold_in(key_of[4], 71), 0)
    return dict(queries=queries, keys_values=keys_values, random_blocks=random_blocks, global_blocks=global_blocks)


def reference(queries, keys_values, random_blocks, global_blocks):
    group_size = HQ // KVH
    q_all = queries.reshape(NBLK, BLOCK, KVH, group_size, HD)
    k_all = keys_values[:, 0].reshape(NBLK, BLOCK, KVH, HD)
    v_all = keys_values[:, 1].reshape(NBLK, BLOCK, KVH, HD)
    own_ids = jnp.arange(NBLK, dtype=jnp.int32)
    window_ids = own_ids[:, None] + jnp.arange(-WIN, WIN + 1, dtype=jnp.int32)[None, :]
    window_ok = (window_ids >= 0) & (window_ids < NBLK)
    lookup = jnp.concatenate([jnp.clip(window_ids, 0, NBLK - 1).astype(jnp.int32),
                              jnp.broadcast_to(global_blocks[None, :], (NBLK, GLOB)).astype(jnp.int32),
                              random_blocks.astype(jnp.int32)], axis=1)
    usable = jnp.concatenate([window_ok, jnp.ones((NBLK, GLOB + RAND), jnp.bool_)], axis=1)
    scaling = HD ** -0.5
    group_count = NBLK // 8

    def one_group(pieces):
        q_part, i_part, u_part = pieces
        key_rows = jnp.take(k_all, i_part, axis=0).astype(jnp.float32)
        value_rows = jnp.take(v_all, i_part, axis=0).astype(jnp.float32)
        scores = jnp.einsum('qbhgd,qjchd->qhgbjc', q_part.astype(jnp.float32), key_rows) * scaling
        scores = jnp.where(u_part[:, None, None, None, :, None], scores, -1e30)
        highest = jnp.max(scores, axis=(4, 5), keepdims=True)
        weights = jnp.exp(scores - highest)
        totals = jnp.sum(weights, axis=(4, 5))
        rounded = lax.optimization_barrier(weights.astype(jnp.bfloat16)).astype(jnp.float32)
        blended = jnp.einsum('qhgbjc,qjchd->qbhgd', rounded, value_rows)
        blended = blended / jnp.transpose(totals, (0, 3, 1, 2))[..., None]
        return blended.astype(jnp.bfloat16).reshape(8 * BLOCK, HQ * HD)

    results = lax.map(one_group, (q_all.reshape((group_count, 8) + q_all.shape[1:]),
                                  lookup.reshape(group_count, 8, KB),
                                  usable.reshape(group_count, 8, KB)))
    return results.reshape(SEQ, HQ * HD)
```

```python
import functools

import jax
import jax.numpy as jnp
from jax import lax
from jax.experimental import pallas as pl
from jax.experimental.pallas import tpu as pltpu
from jax.sharding import Mesh
from jax.sharding import PartitionSpec as P

KVH = 8
HD = 128
BLOCK = 128
WIN = 1
RAND = 3
LOG2E = 1.4426950408889634


def attend_kernel(heads, slots, table_ref, valid_ref, q_ref, pool_ref, out_ref):
    row = pl.program_id(0)
    q_rows = jnp.concatenate([q_ref[0, 0, :, h * HD : (h + 1) * HD] for h in range(heads)], axis=0)
    where = [table_ref[row, j] for j in range(slots)]
    scores = []
    for j in range(slots):
        part = lax.dot_general(
            q_rows, pool_ref[where[j], 0], (((1,), (1,)), ((), ())), preferred_element_type=jnp.float32
        )
        if j in (0, 2 * WIN):
            part = jnp.where(valid_ref[row, j] > 0, part, -1e30)
        scores.append(part)
    scores = jnp.concatenate(scores, axis=1)
    highest = jnp.max(scores, axis=1, keepdims=True)
    factor = HD ** (-0.5) * LOG2E
    weights = jnp.exp2((scores - highest) * factor)
    totals = jnp.sum(weights, axis=1, keepdims=True)
    values = jnp.concatenate([pool_ref[where[j], 1] for j in range(slots)], axis=0)
    blended = jnp.dot(weights.astype(jnp.bfloat16), values, preferred_element_type=jnp.float32)
    blended = (blended / totals).astype(jnp.bfloat16)
    for h in range(heads):
        out_ref[0, 0, :, h * HD : (h + 1) * HD] = blended[h * BLOCK : (h + 1) * BLOCK]


def on_device(queries, keys_values, random_blocks, global_blocks):
    outer, hi, lo = (lax.axis_size(a) for a in ("outer", "hi", "lo"))
    group = outer * lo
    tokens, width = queries.shape
    heads = width // HD // group
    per = tokens // BLOCK
    total = random_blocks.shape[0]
    plane = lax.axis_index("hi")

    moved = keys_values.reshape(per, BLOCK, 2, KVH, HD).transpose(3, 0, 2, 1, 4)
    moved = lax.all_to_all(moved, ("outer", "lo"), split_axis=0, concat_axis=0, tiled=True)
    pool = lax.all_gather(moved, "hi", axis=0, tiled=True).reshape(hi * group * per, 2, BLOCK, HD)
    asked = queries.reshape(tokens, group, heads * HD).transpose(1, 0, 2)
    asked = lax.all_to_all(asked, ("outer", "lo"), split_axis=0, concat_axis=0, tiled=True)
    asked = asked.reshape(group, per, BLOCK, heads * HD)

    def pool_row(block):
        r, rest = block % per, block // per
        x, rest = rest % lo, rest // lo
        z, o = rest % hi, rest // hi
        return ((z * outer + o) * lo + x) * per + r

    own = jnp.arange(group * per, dtype=jnp.int32)
    own_o, own_x, own_r = own // (lo * per), own // per % lo, own % per
    ids = ((own_o * hi + plane) * lo + own_x) * per + own_r
    near = ids[:, None] + jnp.arange(-WIN, WIN + 1, dtype=jnp.int32)[None, :]
    near_ok = ((near >= 0) & (near < total)).astype(jnp.int32)
    glob = jnp.broadcast_to(global_blocks[None, :], (group * per, global_blocks.shape[0]))
    lists = jnp.concatenate([jnp.clip(near, 0, total - 1), glob, random_blocks[ids]], axis=1)
    table = pool_row(lists)
    slots = table.shape[1]

    results = pl.pallas_call(
        functools.partial(attend_kernel, heads, slots),
        grid_spec=pltpu.PrefetchScalarGridSpec(
            num_scalar_prefetch=2,
            grid=(group * per,),
            in_specs=[
                pl.BlockSpec((1, 1, BLOCK, heads * HD), lambda i, *_: (i // per, i % per, 0, 0)),
                pl.BlockSpec(pool.shape, lambda i, *_: (0, 0, 0, 0), pipeline_mode=pl.Buffered(1)),
            ],
            out_specs=pl.BlockSpec((1, 1, BLOCK, heads * HD), lambda i, *_: (i // per, i % per, 0, 0)),
        ),
        out_shape=jax.ShapeDtypeStruct(asked.shape, jnp.bfloat16),
        name="attend",
    )(table, near_ok, asked, pool)
    back = lax.all_to_all(
        results.reshape(group, tokens, heads * HD), ("outer", "lo"), split_axis=0, concat_axis=0, tiled=True
    )
    return back.transpose(1, 0, 2).reshape(tokens, width)


def solution(mesh):
    outer, inner = mesh.shape["outer"], mesh.shape["inner"]
    lo = max(1, KVH // outer)
    fine = Mesh(mesh.devices.reshape(outer, inner // lo, lo), ("outer", "hi", "lo"))
    split = ("outer", "hi", "lo")
    return jax.shard_map(
        on_device,
        mesh=fine,
        in_specs=(P(split, None), P(split, None, None), P(), P()),
        out_specs=P(split, None),
        check_vma=False,
    )
```

```python
import functools

import jax
import jax.numpy as jnp
from jax import lax
from jax.experimental import pallas as pl
from jax.experimental.pallas import tpu as pltpu
from jax.sharding import Mesh
from jax.sharding import PartitionSpec as P

KVH = 8
HD = 128
BLOCK = 128
WIN = 1
LOG2E = 1.4426950408889634
MESH = pl.DeviceIdType.MESH


def fused(
    outer, hi, lo, per, heads, globs, rands,
    random_ref, global_ref, q_ref, kv_ref, out_ref,
    pool, asked, made,
    pool_recv, up_send, down_send, plane_send, q_recv, q_send, o_recv, o_send, local_sem,
):
    group = outer * lo
    width = heads * HD
    total = hi * group * per
    o, z, x = lax.axis_index("outer"), lax.axis_index("hi"), lax.axis_index("lo")
    me = o * lo + x
    has_up, has_down = z < hi - 1, z > 0

    def at(peer):
        return (peer // lo, z, peer % lo)

    def chunk(plane, member):
        return pool.at[pl.ds((plane * group + member) * per, per)]

    def columns(member):
        return pl.ds(pl.multiple_of(member * width, width), width)

    def kv_copy(k, sender, receiver, target):
        return pltpu.make_async_remote_copy(
            src_ref=kv_ref.at[receiver],
            dst_ref=chunk(z, sender),
            send_sem=plane_send.at[k],
            recv_sem=pool_recv.at[z * group + sender],
            device_id=at(target),
            device_id_type=MESH,
        )

    def q_copy(k, sender, receiver, target):
        return pltpu.make_async_remote_copy(
            src_ref=q_ref.at[:, columns(receiver)],
            dst_ref=asked.at[sender],
            send_sem=q_send.at[k],
            recv_sem=q_recv.at[sender],
            device_id=at(target),
            device_id_type=MESH,
        )

    def hop_copy(plane, member, sems, step):
        return pltpu.make_async_remote_copy(
            src_ref=chunk(plane, member),
            dst_ref=chunk(plane, member),
            send_sem=sems.at[plane * group + member],
            recv_sem=pool_recv.at[plane * group + member],
            device_id=(o, z + step, x),
            device_id_type=MESH,
        )

    def out_copy(block, r, sender, target):
        return pltpu.make_async_remote_copy(
            src_ref=made.at[block],
            dst_ref=out_ref.at[pl.ds(pl.multiple_of(r * BLOCK, BLOCK), BLOCK), columns(sender)],
            send_sem=o_send.at[block],
            recv_sem=o_recv.at[sender * per + r],
            device_id=at(target),
            device_id_type=MESH,
        )

    barrier = pltpu.get_barrier_semaphore()
    for k in range(1, group):
        pl.semaphore_signal(barrier, inc=1, device_id=at((me + k) % group), device_id_type=MESH)

    @pl.when(has_up)
    def _():
        pl.semaphore_signal(barrier, inc=1, device_id=(o, z + 1, x), device_id_type=MESH)

    @pl.when(has_down)
    def _():
        pl.semaphore_signal(barrier, inc=1, device_id=(o, z - 1, x), device_id_type=MESH)

    own_kv = pltpu.make_async_copy(kv_ref.at[me], chunk(z, me), local_sem.at[0])
    own_kv.start()
    own_q = pltpu.make_async_copy(q_ref.at[:, columns(me)], asked.at[me], local_sem.at[1])
    own_q.start()
    pl.semaphore_wait(barrier, group - 1 + has_up.astype(jnp.int32) + has_down.astype(jnp.int32))

    for k in range(1, group):
        kv_copy(k, me, (me + k) % group, (me + k) % group).start()
    own_kv.wait()

    def spread(plane, member, up, down):
        if up is not None:

            @pl.when(up)
            def _():
                hop_copy(plane, member, up_send, 1).start()

        if down is not None:

            @pl.when(down)
            def _():
                hop_copy(plane, member, down_send, -1).start()

    spread(z, me, has_up, has_down)
    for k in range(1, group):
        q_copy(k, me, (me + k) % group, (me + k) % group).start()

    def plane_step(k, carry):
        member = (me + group - k) % group
        kv_copy(k, member, me, member).wait_recv()
        spread(z, member, has_up, has_down)
        return carry

    lax.fori_loop(1, group, plane_step, 0)

    def line_step(n, carry):
        away = n // group + 1
        member = (me + group - n % group) % group

        @pl.when(z - away >= 0)
        def _():
            hop_copy(z - away, member, up_send, -1).wait_recv()
            spread(z - away, member, has_up, None)

        @pl.when(z + away < hi)
        def _():
            hop_copy(z + away, member, down_send, 1).wait_recv()
            spread(z + away, member, None, has_down)

        return carry

    lax.fori_loop(0, (hi - 1) * group, line_step, 0)
    own_q.wait()

    def q_wait(k, carry):
        member = (me + group - k) % group
        q_copy(k, member, me, member).wait_recv()
        return carry

    lax.fori_loop(1, group, q_wait, 0)

    def pool_row(block):
        tail = lax.rem(block, lo * per)
        rest = lax.div(block, lo * per)
        return (lax.rem(rest, hi) * outer + lax.div(rest, hi)) * lo * per + tail

    def attend(n):
        member = (me + 1 + n // per) % group
        r = n % per
        block = ((member // lo * hi + z) * lo + member % lo) * per + r
        first = pl.multiple_of(r * BLOCK, BLOCK)
        q_rows = jnp.concatenate(
            [asked[member, pl.ds(first, BLOCK), h * HD : (h + 1) * HD] for h in range(heads)], axis=0
        )
        near = [block + w for w in range(-WIN, WIN + 1)]
        rows = [pool_row(jnp.clip(b, 0, total - 1)) for b in near]
        rows += [pool_row(global_ref[j]) for j in range(globs)]
        rows += [pool_row(random_ref[block, j]) for j in range(rands)]
        scores = []
        for j, row in enumerate(rows):
            part = lax.dot_general(
                q_rows, pool[row, 0], (((1,), (1,)), ((), ())), preferred_element_type=jnp.float32
            )
            if j < 2 * WIN + 1 and j != WIN:
                part = jnp.where((near[j] >= 0) & (near[j] < total), part, -1e30)
            scores.append(part)
        scores = jnp.concatenate(scores, axis=1)
        highest = jnp.max(scores, axis=1, keepdims=True)
        weights = jnp.exp2((scores - highest) * (HD ** (-0.5) * LOG2E))
        totals = jnp.sum(weights, axis=1, keepdims=True)
        values = jnp.concatenate([pool[row, 1] for row in rows], axis=0)
        blended = jnp.dot(weights.astype(jnp.bfloat16), values, preferred_element_type=jnp.float32)
        blended = (blended / totals).astype(jnp.bfloat16)
        for h in range(heads):
            made[n, :, h * HD : (h + 1) * HD] = blended[h * BLOCK : (h + 1) * BLOCK]

    def send(n):
        out_copy(n, n % per, me, (me + 1 + n // per) % group).start()

    blocks = group * per
    away_blocks = blocks - per
    attend(0)

    def attend_step(n, carry):
        attend(n)

        @pl.when(n <= away_blocks)
        def _():
            send(n - 1)

        return carry

    lax.fori_loop(1, blocks, attend_step, 0)
    keeps = [
        pltpu.make_async_copy(
            made.at[away_blocks + r], out_ref.at[pl.ds(r * BLOCK, BLOCK), columns(me)], local_sem.at[2 + r]
        )
        for r in range(per)
    ]

    def plane_done(k, carry):
        peer = (me + k) % group
        kv_copy(k, me, peer, peer).wait_send()
        q_copy(k, me, peer, peer).wait_send()
        return carry

    lax.fori_loop(1, group, plane_done, 0)

    def hops_done(n, carry):
        plane, member = n // group, n % group

        @pl.when(has_up & (plane <= z))
        def _():
            hop_copy(plane, member, up_send, 1).wait_send()

        @pl.when(has_down & (plane >= z))
        def _():
            hop_copy(plane, member, down_send, -1).wait_send()

        return carry

    lax.fori_loop(0, hi * group, hops_done, 0)
    for keep in keeps:
        keep.start()

    def out_done(n, carry):
        r = n % per
        peer = (me + 1 + n // per) % group
        out_copy(n, r, peer, peer).wait_recv()
        out_copy(n, r, me, peer).wait_send()
        return carry

    lax.fori_loop(0, away_blocks, out_done, 0)
    for keep in keeps:
        keep.wait()


def on_device(queries, keys_values, random_blocks, global_blocks):
    outer, hi, lo = (lax.axis_size(a) for a in ("outer", "hi", "lo"))
    group = outer * lo
    tokens, width = queries.shape
    heads = width // HD // group
    per = tokens // BLOCK
    blocks = group * per
    moved = keys_values.reshape(per, BLOCK, 2, KVH, HD).transpose(3, 0, 2, 1, 4)
    dma = pltpu.SemaphoreType.DMA
    return pl.pallas_call(
        functools.partial(
            fused, outer, hi, lo, per, heads, global_blocks.shape[0], random_blocks.shape[1]
        ),
        in_specs=[pl.BlockSpec(memory_space=pltpu.SMEM)] * 2 + [pl.BlockSpec(memory_space=pl.ANY)] * 2,
        out_specs=pl.BlockSpec(memory_space=pl.ANY),
        out_shape=jax.ShapeDtypeStruct((tokens, width), jnp.bfloat16),
        scratch_shapes=[
            pltpu.VMEM((hi * blocks, 2, BLOCK, HD), jnp.bfloat16),
            pltpu.VMEM((group, tokens, heads * HD), jnp.bfloat16),
            pltpu.VMEM((blocks, BLOCK, heads * HD), jnp.bfloat16),
            dma((hi * group,)),
            dma((hi * group,)),
            dma((hi * group,)),
            dma((group,)),
            dma((group,)),
            dma((group,)),
            dma((blocks,)),
            dma((blocks,)),
            dma((2 + per,)),
        ],
        compiler_params=pltpu.CompilerParams(collective_id=0, has_side_effects=True),
        name="attend",
    )(random_blocks, global_blocks, queries, moved)


def solution(mesh):
    outer, inner = mesh.shape["outer"], mesh.shape["inner"]
    lo = max(1, KVH // outer)
    fine = Mesh(mesh.devices.reshape(outer, inner // lo, lo), ("outer", "hi", "lo"))
    split = ("outer", "hi", "lo")
    return jax.shard_map(
        on_device,
        mesh=fine,
        in_specs=(P(split, None), P(split, None, None), P(), P()),
        out_specs=P(split, None),
        check_vma=False,
    )
```

```python
import functools

import jax
import jax.numpy as jnp
from jax import lax
from jax.experimental import pallas as pl
from jax.experimental.pallas import tpu as pltpu
from jax.sharding import Mesh
from jax.sharding import PartitionSpec as P

KVH = 8
HD = 128
BLOCK = 128
WIN = 1
LOG2E = 1.4426950408889634
MESH = pl.DeviceIdType.MESH


def fused(
    outer, hi, lo, per, heads, globs, rands,
    random_ref, global_ref, q_ref, kv_ref, out_ref,
    pool, asked, made,
    pool_recv, up_send, down_send, plane_send, q_recv, q_send, o_recv, o_send, local_sem, go_sem,
):
    group = outer * lo
    width = heads * HD
    total = hi * group * per
    o, z, x = lax.axis_index("outer"), lax.axis_index("hi"), lax.axis_index("lo")
    me = o * lo + x
    has_up, has_down = z < hi - 1, z > 0

    second = o % 2 == 1

    def at(peer):
        return (peer // lo, z, peer % lo)

    def chunk(plane, member):
        return pool.at[pl.ds((plane * group + member) * per, per)]

    def columns(member):
        return pl.ds(pl.multiple_of(member * width, width), width)

    def kv_copy(k, sender, receiver, target):
        return pltpu.make_async_remote_copy(
            src_ref=kv_ref.at[receiver],
            dst_ref=chunk(z, sender),
            send_sem=plane_send.at[k],
            recv_sem=pool_recv.at[z * group + sender],
            device_id=at(target),
            device_id_type=MESH,
        )

    def q_copy(k, sender, receiver, target):
        return pltpu.make_async_remote_copy(
            src_ref=q_ref.at[:, columns(receiver)],
            dst_ref=asked.at[sender],
            send_sem=q_send.at[k],
            recv_sem=q_recv.at[sender],
            device_id=at(target),
            device_id_type=MESH,
        )

    def hop_copy(plane, member, sems, step):
        return pltpu.make_async_remote_copy(
            src_ref=chunk(plane, member),
            dst_ref=chunk(plane, member),
            send_sem=sems.at[plane * group + member],
            recv_sem=pool_recv.at[plane * group + member],
            device_id=(o, z + step, x),
            device_id_type=MESH,
        )

    def out_copy(block, r, sender, target):
        return pltpu.make_async_remote_copy(
            src_ref=made.at[block],
            dst_ref=out_ref.at[pl.ds(pl.multiple_of(r * BLOCK, BLOCK), BLOCK), columns(sender)],
            send_sem=o_send.at[block],
            recv_sem=o_recv.at[sender * per + r],
            device_id=at(target),
            device_id_type=MESH,
        )

    barrier = pltpu.get_barrier_semaphore()
    for k in range(1, group):
        pl.semaphore_signal(barrier, inc=1, device_id=at((me + k) % group), device_id_type=MESH)

    @pl.when(has_up)
    def _():
        pl.semaphore_signal(barrier, inc=1, device_id=(o, z + 1, x), device_id_type=MESH)

    @pl.when(has_down)
    def _():
        pl.semaphore_signal(barrier, inc=1, device_id=(o, z - 1, x), device_id_type=MESH)

    own_kv = pltpu.make_async_copy(kv_ref.at[me], chunk(z, me), local_sem.at[0])
    own_kv.start()
    own_q = pltpu.make_async_copy(q_ref.at[:, columns(me)], asked.at[me], local_sem.at[1])
    own_q.start()
    pl.semaphore_wait(barrier, group - 1 + has_up.astype(jnp.int32) + has_down.astype(jnp.int32))

    for k in range(1, group):
        kv_copy(k, me, (me + k) % group, (me + k) % group).start()
    own_kv.wait()

    def spread(plane, member, up, down):
        if up is not None:

            @pl.when(up)
            def _():
                hop_copy(plane, member, up_send, 1).start()

        if down is not None:

            @pl.when(down)
            def _():
                hop_copy(plane, member, down_send, -1).start()

    for k in range(1, group):
        q_copy(k, me, (me + k) % group, (me + k) % group).start()

    @pl.when(second)
    def _():
        pl.semaphore_wait(go_sem, 1)

    spread(z, me, has_up, has_down)

    def plane_step(k, carry):
        member = (me + group - k) % group
        kv_copy(k, member, me, member).wait_recv()
        spread(z, member, has_up, has_down)
        return carry

    lax.fori_loop(1, group, plane_step, 0)

    def line_step(n, carry):
        away = n // group + 1
        member = (me + group - n % group) % group

        @pl.when(z - away >= 0)
        def _():
            hop_copy(z - away, member, up_send, -1).wait_recv()
            spread(z - away, member, has_up, None)

        @pl.when(z + away < hi)
        def _():
            hop_copy(z + away, member, down_send, 1).wait_recv()
            spread(z + away, member, None, has_down)

        return carry

    lax.fori_loop(0, (hi - 1) * group, line_step, 0)

    @pl.when(jnp.logical_not(second))
    def _():
        pl.semaphore_signal(go_sem, inc=1, device_id=(o + 1, z, x), device_id_type=MESH)

    own_q.wait()

    def q_wait(k, carry):
        member = (me + group - k) % group
        q_copy(k, member, me, member).wait_recv()
        return carry

    lax.fori_loop(1, group, q_wait, 0)

    def pool_row(block):
        tail = lax.rem(block, lo * per)
        rest = lax.div(block, lo * per)
        return (lax.rem(rest, hi) * outer + lax.div(rest, hi)) * lo * per + tail

    def attend(n):
        member = (me + 1 + n // per) % group
        r = n % per
        block = ((member // lo * hi + z) * lo + member % lo) * per + r
        first = pl.multiple_of(r * BLOCK, BLOCK)
        q_rows = jnp.concatenate(
            [asked[member, pl.ds(first, BLOCK), h * HD : (h + 1) * HD] for h in range(heads)], axis=0
        )
        near = [block + w for w in range(-WIN, WIN + 1)]
        rows = [pool_row(jnp.clip(b, 0, total - 1)) for b in near]
        rows += [pool_row(global_ref[j]) for j in range(globs)]
        rows += [pool_row(random_ref[block, j]) for j in range(rands)]
        scores = []
        for j, row in enumerate(rows):
            part = lax.dot_general(
                q_rows, pool[row, 0], (((1,), (1,)), ((), ())), preferred_element_type=jnp.float32
            )
            if j < 2 * WIN + 1 and j != WIN:
                part = jnp.where((near[j] >= 0) & (near[j] < total), part, -1e30)
            scores.append(part)
        scores = jnp.concatenate(scores, axis=1)
        highest = jnp.max(scores, axis=1, keepdims=True)
        weights = jnp.exp2((scores - highest) * (HD ** (-0.5) * LOG2E))
        totals = jnp.sum(weights, axis=1, keepdims=True)
        values = jnp.concatenate([pool[row, 1] for row in rows], axis=0)
        blended = jnp.dot(weights.astype(jnp.bfloat16), values, preferred_element_type=jnp.float32)
        blended = (blended / totals).astype(jnp.bfloat16)
        for h in range(heads):
            made[n, :, h * HD : (h + 1) * HD] = blended[h * BLOCK : (h + 1) * BLOCK]

    def send(n):
        out_copy(n, n % per, me, (me + 1 + n // per) % group).start()

    blocks = group * per
    away_blocks = blocks - per
    attend(0)

    def attend_step(n, carry):
        attend(n)

        @pl.when(n <= away_blocks)
        def _():
            send(n - 1)

        return carry

    lax.fori_loop(1, blocks, attend_step, 0)
    keeps = [
        pltpu.make_async_copy(
            made.at[away_blocks + r], out_ref.at[pl.ds(r * BLOCK, BLOCK), columns(me)], local_sem.at[2 + r]
        )
        for r in range(per)
    ]

    def plane_done(k, carry):
        peer = (me + k) % group
        kv_copy(k, me, peer, peer).wait_send()
        q_copy(k, me, peer, peer).wait_send()
        return carry

    lax.fori_loop(1, group, plane_done, 0)

    def hops_done(n, carry):
        plane, member = n // group, n % group

        @pl.when(has_up & (plane <= z))
        def _():
            hop_copy(plane, member, up_send, 1).wait_send()

        @pl.when(has_down & (plane >= z))
        def _():
            hop_copy(plane, member, down_send, -1).wait_send()

        return carry

    lax.fori_loop(0, hi * group, hops_done, 0)
    for keep in keeps:
        keep.start()

    def out_done(n, carry):
        r = n % per
        peer = (me + 1 + n // per) % group
        out_copy(n, r, peer, peer).wait_recv()
        out_copy(n, r, me, peer).wait_send()
        return carry

    lax.fori_loop(0, away_blocks, out_done, 0)
    for keep in keeps:
        keep.wait()


def on_device(queries, keys_values, random_blocks, global_blocks):
    outer, hi, lo = (lax.axis_size(a) for a in ("outer", "hi", "lo"))
    group = outer * lo
    tokens, width = queries.shape
    heads = width // HD // group
    per = tokens // BLOCK
    blocks = group * per
    moved = keys_values.reshape(per, BLOCK, 2, KVH, HD).transpose(3, 0, 2, 1, 4)
    limit = 2 * (hi * blocks * 2 * BLOCK * HD + 2 * tokens * width) + (12 << 20)
    dma = pltpu.SemaphoreType.DMA
    return pl.pallas_call(
        functools.partial(
            fused, outer, hi, lo, per, heads, global_blocks.shape[0], random_blocks.shape[1]
        ),
        in_specs=[pl.BlockSpec(memory_space=pltpu.SMEM)] * 2 + [pl.BlockSpec(memory_space=pl.ANY)] * 2,
        out_specs=pl.BlockSpec(memory_space=pl.ANY),
        out_shape=jax.ShapeDtypeStruct((tokens, width), jnp.bfloat16),
        scratch_shapes=[
            pltpu.VMEM((hi * blocks, 2, BLOCK, HD), jnp.bfloat16),
            pltpu.VMEM((group, tokens, heads * HD), jnp.bfloat16),
            pltpu.VMEM((blocks, BLOCK, heads * HD), jnp.bfloat16),
            dma((hi * group,)),
            dma((hi * group,)),
            dma((hi * group,)),
            dma((group,)),
            dma((group,)),
            dma((group,)),
            dma((blocks,)),
            dma((blocks,)),
            dma((2 + per,)),
            pltpu.SemaphoreType.REGULAR,
        ],
        compiler_params=pltpu.CompilerParams(collective_id=0, has_side_effects=True, vmem_limit_bytes=limit),
        name="attend",
    )(random_blocks, global_blocks, queries, moved)


def solution(mesh):
    outer, inner = mesh.shape["outer"], mesh.shape["inner"]
    lo = max(1, KVH // outer)
    fine = Mesh(mesh.devices.reshape(outer, inner // lo, lo), ("outer", "hi", "lo"))
    split = ("outer", "hi", "lo")
    return jax.shard_map(
        on_device,
        mesh=fine,
        in_specs=(P(split, None), P(split, None, None), P(), P()),
        out_specs=P(split, None),
        check_vma=False,
    )
```

```python
import functools

import jax
import jax.numpy as jnp
from jax import lax
from jax.experimental import pallas as pl
from jax.experimental.pallas import tpu as pltpu
from jax.sharding import Mesh
from jax.sharding import PartitionSpec as P

KVH = 8
HD = 128
BLOCK = 128
WIN = 1
LOG2E = 1.4426950408889634
MESH = pl.DeviceIdType.MESH


def fused(
    outer, hi, lo, per, heads, globs, rands,
    random_ref, global_ref, q_ref, kv_ref, out_ref,
    pool, asked, made, spare, spare_asked, spare_made,
    pool_recv, up_send, down_send, plane_send, q_recv, q_send, o_recv, o_send, local_sem, go_sem,
    help_send, help_recv, help_q_send, help_q_recv, help_o_send,
):
    group = outer * lo
    width = heads * HD
    total = hi * group * per
    half = per // 2
    o, z, x = lax.axis_index("outer"), lax.axis_index("hi"), lax.axis_index("lo")
    me = o * lo + x
    has_up, has_down = z < hi - 1, z > 0

    second = o % 2 == 1
    first = o % 2 == 0

    def at(peer):
        return (peer // lo, z, peer % lo)

    def chunk(plane, member):
        return pool.at[pl.ds((plane * group + member) * per, per)]

    def columns(member):
        return pl.ds(pl.multiple_of(member * width, width), width)

    def kv_copy(k, sender, receiver, target):
        return pltpu.make_async_remote_copy(
            src_ref=kv_ref.at[receiver],
            dst_ref=chunk(z, sender),
            send_sem=plane_send.at[k],
            recv_sem=pool_recv.at[z * group + sender],
            device_id=at(target),
            device_id_type=MESH,
        )

    def q_copy(k, sender, receiver, target):
        return pltpu.make_async_remote_copy(
            src_ref=q_ref.at[:, columns(receiver)],
            dst_ref=asked.at[sender],
            send_sem=q_send.at[k],
            recv_sem=q_recv.at[sender],
            device_id=at(target),
            device_id_type=MESH,
        )

    def hop_copy(plane, member, sems, step):
        return pltpu.make_async_remote_copy(
            src_ref=chunk(plane, member),
            dst_ref=chunk(plane, member),
            send_sem=sems.at[plane * group + member],
            recv_sem=pool_recv.at[plane * group + member],
            device_id=(o, z + step, x),
            device_id_type=MESH,
        )

    def help_copy(plane, member, step):
        rows = pl.ds((plane * group + member) * per, per)
        return pltpu.make_async_remote_copy(
            src_ref=pool.at[rows],
            dst_ref=spare.at[rows],
            send_sem=help_send.at[plane * group + member],
            recv_sem=help_recv.at[plane * group + member],
            device_id=(o + step, z, x),
            device_id_type=MESH,
        )

    def help_q_copy(step):
        return pltpu.make_async_remote_copy(
            src_ref=asked.at[:, pl.ds(half * BLOCK, half * BLOCK)],
            dst_ref=spare_asked,
            send_sem=help_q_send,
            recv_sem=help_q_recv,
            device_id=(o + step, z, x),
            device_id_type=MESH,
        )

    def place(r, owner):
        return out_ref.at[pl.ds(pl.multiple_of(r * BLOCK, BLOCK), BLOCK), columns(owner)]

    def out_copy(made_ref, sems, block, r, owner, target):
        return pltpu.make_async_remote_copy(
            src_ref=made_ref.at[block],
            dst_ref=place(r, owner),
            send_sem=sems.at[block],
            recv_sem=o_recv.at[owner * per + r],
            device_id=at(target),
            device_id_type=MESH,
        )

    barrier = pltpu.get_barrier_semaphore()
    for k in range(1, group):
        pl.semaphore_signal(barrier, inc=1, device_id=at((me + k) % group), device_id_type=MESH)

    @pl.when(has_up)
    def _():
        pl.semaphore_signal(barrier, inc=1, device_id=(o, z + 1, x), device_id_type=MESH)

    @pl.when(has_down)
    def _():
        pl.semaphore_signal(barrier, inc=1, device_id=(o, z - 1, x), device_id_type=MESH)

    own_kv = pltpu.make_async_copy(kv_ref.at[me], chunk(z, me), local_sem.at[0])
    own_kv.start()
    own_q = pltpu.make_async_copy(q_ref.at[:, columns(me)], asked.at[me], local_sem.at[1])
    own_q.start()
    pl.semaphore_wait(barrier, group - 1 + has_up.astype(jnp.int32) + has_down.astype(jnp.int32))

    for k in range(1, group):
        kv_copy(k, me, (me + k) % group, (me + k) % group).start()
    own_kv.wait()

    def spread(plane, member, up, down):
        @pl.when(second)
        def _():
            help_copy(plane, member, -1).start()

        if up is not None:

            @pl.when(up)
            def _():
                hop_copy(plane, member, up_send, 1).start()

        if down is not None:

            @pl.when(down)
            def _():
                hop_copy(plane, member, down_send, -1).start()

    for k in range(1, group):
        q_copy(k, me, (me + k) % group, (me + k) % group).start()

    def queries_here():
        def q_wait(k, carry):
            member = (me + group - k) % group
            q_copy(k, member, me, member).wait_recv()
            return carry

        lax.fori_loop(1, group, q_wait, 0)
        own_q.wait()

    @pl.when(second)
    def _():
        queries_here()
        help_q_copy(-1).start()
        pl.semaphore_wait(go_sem, 1)

    spread(z, me, has_up, has_down)

    def plane_step(k, carry):
        member = (me + group - k) % group
        kv_copy(k, member, me, member).wait_recv()
        spread(z, member, has_up, has_down)
        return carry

    lax.fori_loop(1, group, plane_step, 0)

    def line_step(n, carry):
        away = n // group + 1
        member = (me + group - n % group) % group

        @pl.when(z - away >= 0)
        def _():
            hop_copy(z - away, member, up_send, -1).wait_recv()
            spread(z - away, member, has_up, None)

        @pl.when(z + away < hi)
        def _():
            hop_copy(z + away, member, down_send, 1).wait_recv()
            spread(z + away, member, None, has_down)

        return carry

    lax.fori_loop(0, (hi - 1) * group, line_step, 0)

    @pl.when(first)
    def _():
        pl.semaphore_signal(go_sem, inc=1, device_id=(o + 1, z, x), device_id_type=MESH)
        queries_here()

    def pool_row(block):
        tail = lax.rem(block, lo * per)
        rest = lax.div(block, lo * per)
        return (lax.rem(rest, hi) * outer + lax.div(rest, hi)) * lo * per + tail

    def attend(n, count, r0, pool, asked, made):
        member = (me + 1 + n // count) % group
        i = n % count
        block = ((member // lo * hi + z) * lo + member % lo) * per + r0 + i
        start = pl.multiple_of(i * BLOCK, BLOCK)
        q_rows = jnp.concatenate(
            [asked[member, pl.ds(start, BLOCK), h * HD : (h + 1) * HD] for h in range(heads)], axis=0
        )
        near = [block + w for w in range(-WIN, WIN + 1)]
        rows = [pool_row(jnp.clip(b, 0, total - 1)) for b in near]
        rows += [pool_row(global_ref[j]) for j in range(globs)]
        rows += [pool_row(random_ref[block, j]) for j in range(rands)]
        scores = []
        for j, row in enumerate(rows):
            part = lax.dot_general(
                q_rows, pool[row, 0], (((1,), (1,)), ((), ())), preferred_element_type=jnp.float32
            )
            if j < 2 * WIN + 1 and j != WIN:
                part = jnp.where((near[j] >= 0) & (near[j] < total), part, -1e30)
            scores.append(part)
        scores = jnp.concatenate(scores, axis=1)
        highest = jnp.max(scores, axis=1, keepdims=True)
        weights = jnp.exp2((scores - highest) * (HD ** (-0.5) * LOG2E))
        totals = jnp.sum(weights, axis=1, keepdims=True)
        values = jnp.concatenate([pool[row, 1] for row in rows], axis=0)
        blended = jnp.dot(weights.astype(jnp.bfloat16), values, preferred_element_type=jnp.float32)
        blended = (blended / totals).astype(jnp.bfloat16)
        for h in range(heads):
            made[n, :, h * HD : (h + 1) * HD] = blended[h * BLOCK : (h + 1) * BLOCK]

    def run(owner, count, r0, pool, asked, made, sems):
        away = (group - 1) * count
        attend(0, count, r0, pool, asked, made)

        def attend_step(n, carry):
            attend(n, count, r0, pool, asked, made)

            @pl.when(n <= away)
            def _():
                b = n - 1
                out_copy(made, sems, b, r0 + b % count, owner, (me + 1 + b // count) % group).start()

            return carry

        lax.fori_loop(1, group * count, attend_step, 0)

    def keep(owner, count, r0, made, sem):
        copies = [
            pltpu.make_async_copy(
                made.at[(group - 1) * count + i], place(r0 + i, owner), local_sem.at[sem + i]
            )
            for i in range(count)
        ]
        for copy in copies:
            copy.start()
        for copy in copies:
            copy.wait()

    def sent(owner, count, r0, made, sems):
        def step(b, carry):
            out_copy(made, sems, b, r0 + b % count, owner, (me + 1 + b // count) % group).wait_send()
            return carry

        lax.fori_loop(0, (group - 1) * count, step, 0)

    @pl.when(first)
    def _():
        run(me, per, 0, pool, asked, made, o_send)

        def help_wait(n, carry):
            help_copy(n // group, n % group, 1).wait_recv()
            return carry

        help_q_copy(1).wait_recv()
        lax.fori_loop(0, hi * group, help_wait, 0)
        run(me + lo, half, half, spare, spare_asked, spare_made, help_o_send)

    @pl.when(second)
    def _():
        run(me, half, 0, pool, asked, made, o_send)

    def plane_done(k, carry):
        peer = (me + k) % group
        kv_copy(k, me, peer, peer).wait_send()
        q_copy(k, me, peer, peer).wait_send()
        return carry

    lax.fori_loop(1, group, plane_done, 0)

    def hops_done(n, carry):
        plane, member = n // group, n % group

        @pl.when(has_up & (plane <= z))
        def _():
            hop_copy(plane, member, up_send, 1).wait_send()

        @pl.when(has_down & (plane >= z))
        def _():
            hop_copy(plane, member, down_send, -1).wait_send()

        @pl.when(second)
        def _():
            help_copy(plane, member, -1).wait_send()

        return carry

    lax.fori_loop(0, hi * group, hops_done, 0)

    @pl.when(first)
    def _():
        keep(me, per, 0, made, 2)
        keep(me + lo, half, half, spare_made, 2 + per)
        sent(me, per, 0, made, o_send)
        sent(me + lo, half, half, spare_made, help_o_send)

    @pl.when(second)
    def _():
        help_q_copy(-1).wait_send()
        keep(me, half, 0, made, 2)
        sent(me, half, 0, made, o_send)

    def out_done(n, carry):
        owner, r = n // per, n % per
        here_first = (owner == me) | ((owner == me + lo) & (r >= half))
        here_second = (owner == me) & (r < half)

        @pl.when((first & jnp.logical_not(here_first)) | (second & jnp.logical_not(here_second)))
        def _():
            out_copy(made, o_send, 0, r, owner, (me + 1) % group).wait_recv()

        return carry

    lax.fori_loop(0, group * per, out_done, 0)


def on_device(queries, keys_values, random_blocks, global_blocks):
    outer, hi, lo = (lax.axis_size(a) for a in ("outer", "hi", "lo"))
    group = outer * lo
    tokens, width = queries.shape
    heads = width // HD // group
    per = tokens // BLOCK
    blocks = group * per
    moved = keys_values.reshape(per, BLOCK, 2, KVH, HD).transpose(3, 0, 2, 1, 4)
    limit = 2 * (hi * blocks * 4 * BLOCK * HD + 3 * tokens * width) + (12 << 20)
    dma = pltpu.SemaphoreType.DMA
    return pl.pallas_call(
        functools.partial(
            fused, outer, hi, lo, per, heads, global_blocks.shape[0], random_blocks.shape[1]
        ),
        in_specs=[pl.BlockSpec(memory_space=pltpu.SMEM)] * 2 + [pl.BlockSpec(memory_space=pl.ANY)] * 2,
        out_specs=pl.BlockSpec(memory_space=pl.ANY),
        out_shape=jax.ShapeDtypeStruct((tokens, width), jnp.bfloat16),
        scratch_shapes=[
            pltpu.VMEM((hi * blocks, 2, BLOCK, HD), jnp.bfloat16),
            pltpu.VMEM((group, tokens, heads * HD), jnp.bfloat16),
            pltpu.VMEM((blocks, BLOCK, heads * HD), jnp.bfloat16),
            pltpu.VMEM((hi * blocks, 2, BLOCK, HD), jnp.bfloat16),
            pltpu.VMEM((group, tokens // 2, heads * HD), jnp.bfloat16),
            pltpu.VMEM((blocks // 2, BLOCK, heads * HD), jnp.bfloat16),
            dma((hi * group,)),
            dma((hi * group,)),
            dma((hi * group,)),
            dma((group,)),
            dma((group,)),
            dma((group,)),
            dma((blocks,)),
            dma((blocks,)),
            dma((2 + per + per // 2,)),
            pltpu.SemaphoreType.REGULAR,
            dma((hi * group,)),
            dma((hi * group,)),
            dma,
            dma,
            dma((blocks // 2,)),
        ],
        compiler_params=pltpu.CompilerParams(collective_id=0, has_side_effects=True, vmem_limit_bytes=limit),
        name="attend",
    )(random_blocks, global_blocks, queries, moved)


def solution(mesh):
    outer, inner = mesh.shape["outer"], mesh.shape["inner"]
    lo = max(1, KVH // outer)
    fine = Mesh(mesh.devices.reshape(outer, inner // lo, lo), ("outer", "hi", "lo"))
    split = ("outer", "hi", "lo")
    return jax.shard_map(
        on_device,
        mesh=fine,
        in_specs=(P(split, None), P(split, None, None), P(), P()),
        out_specs=P(split, None),
        check_vma=False,
    )
```

```python
import functools

import jax
import jax.numpy as jnp
from jax import lax
from jax.experimental import pallas as pl
from jax.experimental.pallas import tpu as pltpu
from jax.sharding import Mesh
from jax.sharding import PartitionSpec as P

KVH = 8
HD = 128
BLOCK = 128
WIN = 1
LOG2E = 1.4426950408889634
MESH = pl.DeviceIdType.MESH


def fused(
    outer, hi, lo, per, heads, globs, rands,
    random_ref, global_ref, q_ref, kv_ref, out_ref,
    pool, asked, made, spare, spare_asked, spare_made,
    pool_recv, up_send, down_send, plane_send, q_recv, q_send, o_recv, o_send, local_sem, go_sem,
    help_send, help_recv, help_q_send, help_q_recv, help_o_send,
):
    group = outer * lo
    width = heads * HD
    total = hi * group * per
    half = per // 2
    o, z, x = lax.axis_index("outer"), lax.axis_index("hi"), lax.axis_index("lo")
    me = o * lo + x
    has_up, has_down = z < hi - 1, z > 0

    second = o % 2 == 1
    first = o % 2 == 0

    def at(peer):
        return (peer // lo, z, peer % lo)

    def chunk(plane, member):
        return pool.at[pl.ds((plane * group + member) * per, per)]

    def columns(member):
        return pl.ds(pl.multiple_of(member * width, width), width)

    def kv_copy(k, sender, receiver, target):
        return pltpu.make_async_remote_copy(
            src_ref=kv_ref.at[receiver],
            dst_ref=chunk(z, sender),
            send_sem=plane_send.at[k],
            recv_sem=pool_recv.at[z * group + sender],
            device_id=at(target),
            device_id_type=MESH,
        )

    def q_copy(k, sender, receiver, target):
        return pltpu.make_async_remote_copy(
            src_ref=q_ref.at[:, columns(receiver)],
            dst_ref=asked.at[sender],
            send_sem=q_send.at[k],
            recv_sem=q_recv.at[sender],
            device_id=at(target),
            device_id_type=MESH,
        )

    def hop_copy(plane, member, sems, step):
        return pltpu.make_async_remote_copy(
            src_ref=chunk(plane, member),
            dst_ref=chunk(plane, member),
            send_sem=sems.at[plane * group + member],
            recv_sem=pool_recv.at[plane * group + member],
            device_id=(o, z + step, x),
            device_id_type=MESH,
        )

    def help_copy(plane, member, step):
        rows = pl.ds((plane * group + member) * per, per)
        return pltpu.make_async_remote_copy(
            src_ref=pool.at[rows],
            dst_ref=spare.at[rows],
            send_sem=help_send.at[plane * group + member],
            recv_sem=help_recv.at[plane * group + member],
            device_id=(o + step, z, x),
            device_id_type=MESH,
        )

    def help_q_copy(step):
        return pltpu.make_async_remote_copy(
            src_ref=asked.at[:, pl.ds(half * BLOCK, half * BLOCK)],
            dst_ref=spare_asked,
            send_sem=help_q_send,
            recv_sem=help_q_recv,
            device_id=(o + step, z, x),
            device_id_type=MESH,
        )

    def place(r, owner):
        return out_ref.at[pl.ds(pl.multiple_of(r * BLOCK, BLOCK), BLOCK), columns(owner)]

    def out_copy(made_ref, sems, block, r, owner, target):
        return pltpu.make_async_remote_copy(
            src_ref=made_ref.at[block],
            dst_ref=place(r, owner),
            send_sem=sems.at[block],
            recv_sem=o_recv.at[owner * per + r],
            device_id=at(target),
            device_id_type=MESH,
        )

    barrier = pltpu.get_barrier_semaphore()
    for k in range(1, group):
        pl.semaphore_signal(barrier, inc=1, device_id=at((me + k) % group), device_id_type=MESH)

    @pl.when(has_up)
    def _():
        pl.semaphore_signal(barrier, inc=1, device_id=(o, z + 1, x), device_id_type=MESH)

    @pl.when(has_down)
    def _():
        pl.semaphore_signal(barrier, inc=1, device_id=(o, z - 1, x), device_id_type=MESH)

    own_kv = pltpu.make_async_copy(kv_ref.at[me], chunk(z, me), local_sem.at[0])
    own_kv.start()
    own_q = pltpu.make_async_copy(q_ref.at[:, columns(me)], asked.at[me], local_sem.at[1])
    own_q.start()
    pl.semaphore_wait(barrier, group - 1 + has_up.astype(jnp.int32) + has_down.astype(jnp.int32))

    for k in range(1, group):
        kv_copy(k, me, (me + k) % group, (me + k) % group).start()
    own_kv.wait()

    def spread(plane, member, up, down):
        @pl.when(second)
        def _():
            help_copy(plane, member, -1).start()

        if up is not None:

            @pl.when(up)
            def _():
                hop_copy(plane, member, up_send, 1).start()

        if down is not None:

            @pl.when(down)
            def _():
                hop_copy(plane, member, down_send, -1).start()

    for k in range(1, group):
        q_copy(k, me, (me + k) % group, (me + k) % group).start()

    def queries_here():
        def q_wait(k, carry):
            member = (me + group - k) % group
            q_copy(k, member, me, member).wait_recv()
            return carry

        lax.fori_loop(1, group, q_wait, 0)
        own_q.wait()

    spread(z, me, has_up, has_down)

    def plane_step(k, carry):
        member = (me + group - k) % group
        kv_copy(k, member, me, member).wait_recv()
        spread(z, member, has_up, has_down)
        return carry

    lax.fori_loop(1, group, plane_step, 0)

    @pl.when(second)
    def _():
        queries_here()
        help_q_copy(-1).start()
        pl.semaphore_wait(go_sem, 1)

    def line_step(n, carry):
        away = n // group + 1

        @pl.when(first & (n == (hi - 1) * group - 3))
        def _():
            pl.semaphore_signal(go_sem, inc=1, device_id=(o + 1, z, x), device_id_type=MESH)

        member = (me + group - n % group) % group

        @pl.when(z - away >= 0)
        def _():
            hop_copy(z - away, member, up_send, -1).wait_recv()
            spread(z - away, member, has_up, None)

        @pl.when(z + away < hi)
        def _():
            hop_copy(z + away, member, down_send, 1).wait_recv()
            spread(z + away, member, None, has_down)

        return carry

    lax.fori_loop(0, (hi - 1) * group, line_step, 0)

    @pl.when(first)
    def _():
        queries_here()

    def pool_row(block):
        tail = lax.rem(block, lo * per)
        rest = lax.div(block, lo * per)
        return (lax.rem(rest, hi) * outer + lax.div(rest, hi)) * lo * per + tail

    def attend(n, count, r0, pool, asked, made):
        member = (me + 1 + n // count) % group
        i = n % count
        block = ((member // lo * hi + z) * lo + member % lo) * per + r0 + i
        start = pl.multiple_of(i * BLOCK, BLOCK)
        q_rows = jnp.concatenate(
            [asked[member, pl.ds(start, BLOCK), h * HD : (h + 1) * HD] for h in range(heads)], axis=0
        )
        near = [block + w for w in range(-WIN, WIN + 1)]
        rows = [pool_row(jnp.clip(b, 0, total - 1)) for b in near]
        rows += [pool_row(global_ref[j]) for j in range(globs)]
        rows += [pool_row(random_ref[block, j]) for j in range(rands)]
        scores = []
        for j, row in enumerate(rows):
            part = lax.dot_general(
                q_rows, pool[row, 0], (((1,), (1,)), ((), ())), preferred_element_type=jnp.float32
            )
            if j < 2 * WIN + 1 and j != WIN:
                part = jnp.where((near[j] >= 0) & (near[j] < total), part, -1e30)
            scores.append(part)
        scores = jnp.concatenate(scores, axis=1)
        highest = jnp.max(scores, axis=1, keepdims=True)
        weights = jnp.exp2((scores - highest) * (HD ** (-0.5) * LOG2E))
        totals = jnp.sum(weights, axis=1, keepdims=True)
        values = jnp.concatenate([pool[row, 1] for row in rows], axis=0)
        blended = jnp.dot(weights.astype(jnp.bfloat16), values, preferred_element_type=jnp.float32)
        blended = (blended / totals).astype(jnp.bfloat16)
        for h in range(heads):
            made[n, :, h * HD : (h + 1) * HD] = blended[h * BLOCK : (h + 1) * BLOCK]

    def run(owner, count, r0, pool, asked, made, sems):
        away = (group - 1) * count
        attend(0, count, r0, pool, asked, made)

        def attend_step(n, carry):
            attend(n, count, r0, pool, asked, made)

            @pl.when(n <= away)
            def _():
                b = n - 1
                out_copy(made, sems, b, r0 + b % count, owner, (me + 1 + b // count) % group).start()

            return carry

        lax.fori_loop(1, group * count, attend_step, 0)

    def keep(owner, count, r0, made, sem):
        copies = [
            pltpu.make_async_copy(
                made.at[(group - 1) * count + i], place(r0 + i, owner), local_sem.at[sem + i]
            )
            for i in range(count)
        ]
        for copy in copies:
            copy.start()
        for copy in copies:
            copy.wait()

    def sent(owner, count, r0, made, sems):
        def step(b, carry):
            out_copy(made, sems, b, r0 + b % count, owner, (me + 1 + b // count) % group).wait_send()
            return carry

        lax.fori_loop(0, (group - 1) * count, step, 0)

    @pl.when(first)
    def _():
        run(me, per, 0, pool, asked, made, o_send)

        def help_wait(n, carry):
            help_copy(n // group, n % group, 1).wait_recv()
            return carry

        help_q_copy(1).wait_recv()
        lax.fori_loop(0, hi * group, help_wait, 0)
        run(me + lo, half, half, spare, spare_asked, spare_made, help_o_send)

    @pl.when(second)
    def _():
        run(me, half, 0, pool, asked, made, o_send)

    def plane_done(k, carry):
        peer = (me + k) % group
        kv_copy(k, me, peer, peer).wait_send()
        q_copy(k, me, peer, peer).wait_send()
        return carry

    lax.fori_loop(1, group, plane_done, 0)

    def hops_done(n, carry):
        plane, member = n // group, n % group

        @pl.when(has_up & (plane <= z))
        def _():
            hop_copy(plane, member, up_send, 1).wait_send()

        @pl.when(has_down & (plane >= z))
        def _():
            hop_copy(plane, member, down_send, -1).wait_send()

        @pl.when(second)
        def _():
            help_copy(plane, member, -1).wait_send()

        return carry

    lax.fori_loop(0, hi * group, hops_done, 0)

    @pl.when(first)
    def _():
        keep(me, per, 0, made, 2)
        keep(me + lo, half, half, spare_made, 2 + per)
        sent(me, per, 0, made, o_send)
        sent(me + lo, half, half, spare_made, help_o_send)

    @pl.when(second)
    def _():
        help_q_copy(-1).wait_send()
        keep(me, half, 0, made, 2)
        sent(me, half, 0, made, o_send)

    def out_done(n, carry):
        owner, r = n // per, n % per
        here_first = (owner == me) | ((owner == me + lo) & (r >= half))
        here_second = (owner == me) & (r < half)

        @pl.when((first & jnp.logical_not(here_first)) | (second & jnp.logical_not(here_second)))
        def _():
            out_copy(made, o_send, 0, r, owner, (me + 1) % group).wait_recv()

        return carry

    lax.fori_loop(0, group * per, out_done, 0)


def on_device(queries, keys_values, random_blocks, global_blocks):
    outer, hi, lo = (lax.axis_size(a) for a in ("outer", "hi", "lo"))
    group = outer * lo
    tokens, width = queries.shape
    heads = width // HD // group
    per = tokens // BLOCK
    blocks = group * per
    moved = keys_values.reshape(per, BLOCK, 2, KVH, HD).transpose(3, 0, 2, 1, 4)
    limit = 2 * (hi * blocks * 4 * BLOCK * HD + 3 * tokens * width) + (12 << 20)
    dma = pltpu.SemaphoreType.DMA
    return pl.pallas_call(
        functools.partial(
            fused, outer, hi, lo, per, heads, global_blocks.shape[0], random_blocks.shape[1]
        ),
        in_specs=[pl.BlockSpec(memory_space=pltpu.SMEM)] * 2 + [pl.BlockSpec(memory_space=pl.ANY)] * 2,
        out_specs=pl.BlockSpec(memory_space=pl.ANY),
        out_shape=jax.ShapeDtypeStruct((tokens, width), jnp.bfloat16),
        scratch_shapes=[
            pltpu.VMEM((hi * blocks, 2, BLOCK, HD), jnp.bfloat16),
            pltpu.VMEM((group, tokens, heads * HD), jnp.bfloat16),
            pltpu.VMEM((blocks, BLOCK, heads * HD), jnp.bfloat16),
            pltpu.VMEM((hi * blocks, 2, BLOCK, HD), jnp.bfloat16),
            pltpu.VMEM((group, tokens // 2, heads * HD), jnp.bfloat16),
            pltpu.VMEM((blocks // 2, BLOCK, heads * HD), jnp.bfloat16),
            dma((hi * group,)),
            dma((hi * group,)),
            dma((hi * group,)),
            dma((group,)),
            dma((group,)),
            dma((group,)),
            dma((blocks,)),
            dma((blocks,)),
            dma((2 + per + per // 2,)),
            pltpu.SemaphoreType.REGULAR,
            dma((hi * group,)),
            dma((hi * group,)),
            dma,
            dma,
            dma((blocks // 2,)),
        ],
        compiler_params=pltpu.CompilerParams(collective_id=0, has_side_effects=True, vmem_limit_bytes=limit),
        name="attend",
    )(random_blocks, global_blocks, queries, moved)


def solution(mesh):
    outer, inner = mesh.shape["outer"], mesh.shape["inner"]
    lo = max(1, KVH // outer)
    fine = Mesh(mesh.devices.reshape(outer, inner // lo, lo), ("outer", "hi", "lo"))
    split = ("outer", "hi", "lo")
    return jax.shard_map(
        on_device,
        mesh=fine,
        in_specs=(P(split, None), P(split, None, None), P(), P()),
        out_specs=P(split, None),
        check_vma=False,
    )
```

```python
import functools

import jax
import jax.numpy as jnp
from jax import lax
from jax.experimental import pallas as pl
from jax.experimental.pallas import tpu as pltpu
from jax.sharding import Mesh
from jax.sharding import PartitionSpec as P

KVH = 8
HD = 128
BLOCK = 128
WIN = 1
LOG2E = 1.4426950408889634
MESH = pl.DeviceIdType.MESH


def fused(
    outer, hi, lo, per, heads, globs, rands,
    random_ref, global_ref, q_ref, kv_ref, out_ref,
    pool, asked, made, spare, spare_asked, spare_made,
    pool_recv, up_send, down_send, plane_send, q_recv, q_send, o_recv, o_send, local_sem, go_sem,
    help_send, help_recv, help_q_send, help_q_recv, help_o_send,
):
    group = outer * lo
    width = heads * HD
    total = hi * group * per
    half = per // 2
    o, z, x = lax.axis_index("outer"), lax.axis_index("hi"), lax.axis_index("lo")
    me = o * lo + x
    has_up, has_down = z < hi - 1, z > 0

    second = o % 2 == 1
    first = o % 2 == 0

    def at(peer):
        return (peer // lo, z, peer % lo)

    def chunk(plane, member):
        return pool.at[pl.ds((plane * group + member) * per, per)]

    def columns(member):
        return pl.ds(pl.multiple_of(member * width, width), width)

    def kv_copy(k, sender, receiver, target):
        return pltpu.make_async_remote_copy(
            src_ref=kv_ref.at[receiver],
            dst_ref=chunk(z, sender),
            send_sem=plane_send.at[k],
            recv_sem=pool_recv.at[z * group + sender],
            device_id=at(target),
            device_id_type=MESH,
        )

    def q_copy(k, sender, receiver, target):
        return pltpu.make_async_remote_copy(
            src_ref=q_ref.at[:, columns(receiver)],
            dst_ref=asked.at[sender],
            send_sem=q_send.at[k],
            recv_sem=q_recv.at[sender],
            device_id=at(target),
            device_id_type=MESH,
        )

    def hop_copy(plane, member, sems, step):
        return pltpu.make_async_remote_copy(
            src_ref=chunk(plane, member),
            dst_ref=chunk(plane, member),
            send_sem=sems.at[plane * group + member],
            recv_sem=pool_recv.at[plane * group + member],
            device_id=(o, z + step, x),
            device_id_type=MESH,
        )

    def help_copy(plane, member, step):
        rows = pl.ds((plane * group + member) * per, per)
        return pltpu.make_async_remote_copy(
            src_ref=pool.at[rows],
            dst_ref=spare.at[rows],
            send_sem=help_send.at[plane * group + member],
            recv_sem=help_recv.at[plane * group + member],
            device_id=(o + step, z, x),
            device_id_type=MESH,
        )

    def help_q_copy(step):
        return pltpu.make_async_remote_copy(
            src_ref=asked.at[:, pl.ds(half * BLOCK, half * BLOCK)],
            dst_ref=spare_asked,
            send_sem=help_q_send,
            recv_sem=help_q_recv,
            device_id=(o + step, z, x),
            device_id_type=MESH,
        )

    def place(r, owner):
        return out_ref.at[pl.ds(pl.multiple_of(r * BLOCK, BLOCK), BLOCK), columns(owner)]

    def out_copy(made_ref, sems, block, r, owner, target):
        return pltpu.make_async_remote_copy(
            src_ref=made_ref.at[block],
            dst_ref=place(r, owner),
            send_sem=sems.at[block],
            recv_sem=o_recv.at[owner * per + r],
            device_id=at(target),
            device_id_type=MESH,
        )

    barrier = pltpu.get_barrier_semaphore()
    for k in range(1, group):
        pl.semaphore_signal(barrier, inc=1, device_id=at((me + k) % group), device_id_type=MESH)

    @pl.when(has_up)
    def _():
        pl.semaphore_signal(barrier, inc=1, device_id=(o, z + 1, x), device_id_type=MESH)

    @pl.when(has_down)
    def _():
        pl.semaphore_signal(barrier, inc=1, device_id=(o, z - 1, x), device_id_type=MESH)

    own_kv = pltpu.make_async_copy(kv_ref.at[me], chunk(z, me), local_sem.at[0])
    own_kv.start()
    own_q = pltpu.make_async_copy(q_ref.at[:, columns(me)], asked.at[me], local_sem.at[1])
    own_q.start()
    pl.semaphore_wait(barrier, group - 1 + has_up.astype(jnp.int32) + has_down.astype(jnp.int32))

    for k in range(1, group):
        kv_copy(k, me, (me + k) % group, (me + k) % group).start()
    own_kv.wait()

    def spread(plane, member, up, down):
        @pl.when(second)
        def _():
            help_copy(plane, member, -1).start()

        if up is not None:

            @pl.when(up)
            def _():
                hop_copy(plane, member, up_send, 1).start()

        if down is not None:

            @pl.when(down)
            def _():
                hop_copy(plane, member, down_send, -1).start()

    for k in range(1, group):
        q_copy(k, me, (me + k) % group, (me + k) % group).start()

    def queries_here():
        def q_wait(k, carry):
            member = (me + group - k) % group
            q_copy(k, member, me, member).wait_recv()
            return carry

        lax.fori_loop(1, group, q_wait, 0)
        own_q.wait()

    spread(z, me, has_up, has_down)

    def plane_step(k, carry):
        member = (me + group - k) % group
        kv_copy(k, member, me, member).wait_recv()
        spread(z, member, has_up, has_down)
        return carry

    lax.fori_loop(1, group, plane_step, 0)

    @pl.when(second)
    def _():
        queries_here()
        help_q_copy(-1).start()
        pl.semaphore_wait(go_sem, 1)

    def line_step(n, carry):
        away = n // group + 1

        @pl.when(first & (n == (hi - 1) * group - 3))
        def _():
            pl.semaphore_signal(go_sem, inc=1, device_id=(o + 1, z, x), device_id_type=MESH)

        member = (me + group - n % group) % group

        @pl.when(z - away >= 0)
        def _():
            hop_copy(z - away, member, up_send, -1).wait_recv()
            spread(z - away, member, has_up, None)

        @pl.when(z + away < hi)
        def _():
            hop_copy(z + away, member, down_send, 1).wait_recv()
            spread(z + away, member, None, has_down)

        return carry

    lax.fori_loop(0, (hi - 1) * group, line_step, 0)

    @pl.when(first)
    def _():
        queries_here()

    def pool_row(block):
        tail = lax.rem(block, lo * per)
        rest = lax.div(block, lo * per)
        return (lax.rem(rest, hi) * outer + lax.div(rest, hi)) * lo * per + tail

    def attend(n, count, r0, pool, asked, made):
        member = (me + 1 + n // count) % group
        i = n % count
        block = ((member // lo * hi + z) * lo + member % lo) * per + r0 + i
        start = pl.multiple_of(i * BLOCK, BLOCK)
        q_rows = jnp.concatenate(
            [asked[member, pl.ds(start, BLOCK), h * HD : (h + 1) * HD] for h in range(heads)], axis=0
        )
        near = [block + w for w in range(-WIN, WIN + 1)]
        rows = [pool_row(jnp.clip(b, 0, total - 1)) for b in near]
        rows += [pool_row(global_ref[j]) for j in range(globs)]
        rows += [pool_row(random_ref[block, j]) for j in range(rands)]
        scores = []
        for j, row in enumerate(rows):
            part = lax.dot_general(
                pool[row, 0], q_rows, (((1,), (1,)), ((), ())), preferred_element_type=jnp.float32
            )
            if j < 2 * WIN + 1 and j != WIN:
                part = jnp.where((near[j] >= 0) & (near[j] < total), part, -1e30)
            scores.append(part)
        scores = jnp.concatenate(scores, axis=0)
        highest = jnp.max(scores, axis=0, keepdims=True)
        weights = jnp.exp2((scores - highest) * (HD ** (-0.5) * LOG2E))
        totals = jnp.sum(weights, axis=0, keepdims=True)
        values = jnp.concatenate([pool[row, 1] for row in rows], axis=0)
        blended = lax.dot_general(
            values,
            weights.astype(jnp.bfloat16),
            (((0,), (0,)), ((), ())),
            preferred_element_type=jnp.float32,
        )
        blended = blended / totals
        for h in range(heads):
            made[n, :, h * HD : (h + 1) * HD] = blended[:, h * BLOCK : (h + 1) * BLOCK].T.astype(jnp.bfloat16)

    def run(owner, count, r0, pool, asked, made, sems):
        away = (group - 1) * count

        def pair_step(m, carry):
            attend(2 * m, count, r0, pool, asked, made)
            attend(2 * m + 1, count, r0, pool, asked, made)

            @pl.when(m > 0)
            def _():
                for b in (2 * m - 2, 2 * m - 1):
                    send(b, owner, count, r0, made, sems)

            return carry

        lax.fori_loop(0, group * count // 2, pair_step, 0)

    def send(b, owner, count, r0, made, sems):
        out_copy(made, sems, b, r0 + b % count, owner, (me + 1 + b // count) % group).start()

    def last(owner, count, r0, made, sems):
        for b in range(group * count - 2, (group - 1) * count):
            send(b, owner, count, r0, made, sems)

    def keep(owner, count, r0, made, sem):
        copies = [
            pltpu.make_async_copy(
                made.at[(group - 1) * count + i], place(r0 + i, owner), local_sem.at[sem + i]
            )
            for i in range(count)
        ]
        for copy in copies:
            copy.start()
        for copy in copies:
            copy.wait()

    def sent(owner, count, r0, made, sems):
        def step(b, carry):
            out_copy(made, sems, b, r0 + b % count, owner, (me + 1 + b // count) % group).wait_send()
            return carry

        lax.fori_loop(0, (group - 1) * count, step, 0)

    @pl.when(first)
    def _():
        run(me, per, 0, pool, asked, made, o_send)

        def help_wait(n, carry):
            help_copy(n // group, n % group, 1).wait_recv()
            return carry

        help_q_copy(1).wait_recv()
        lax.fori_loop(0, hi * group, help_wait, 0)
        run(me + lo, half, half, spare, spare_asked, spare_made, help_o_send)

    @pl.when(second)
    def _():
        run(me, half, 0, pool, asked, made, o_send)

    def plane_done(k, carry):
        peer = (me + k) % group
        kv_copy(k, me, peer, peer).wait_send()
        q_copy(k, me, peer, peer).wait_send()
        return carry

    lax.fori_loop(1, group, plane_done, 0)

    def hops_done(n, carry):
        plane, member = n // group, n % group

        @pl.when(has_up & (plane <= z))
        def _():
            hop_copy(plane, member, up_send, 1).wait_send()

        @pl.when(has_down & (plane >= z))
        def _():
            hop_copy(plane, member, down_send, -1).wait_send()

        @pl.when(second)
        def _():
            help_copy(plane, member, -1).wait_send()

        return carry

    lax.fori_loop(0, hi * group, hops_done, 0)

    @pl.when(first)
    def _():
        last(me, per, 0, made, o_send)
        last(me + lo, half, half, spare_made, help_o_send)
        keep(me, per, 0, made, 2)
        keep(me + lo, half, half, spare_made, 2 + per)
        sent(me, per, 0, made, o_send)
        sent(me + lo, half, half, spare_made, help_o_send)

    @pl.when(second)
    def _():
        help_q_copy(-1).wait_send()
        last(me, half, 0, made, o_send)
        keep(me, half, 0, made, 2)
        sent(me, half, 0, made, o_send)

    def out_done(n, carry):
        owner, r = n // per, n % per
        here_first = (owner == me) | ((owner == me + lo) & (r >= half))
        here_second = (owner == me) & (r < half)

        @pl.when((first & jnp.logical_not(here_first)) | (second & jnp.logical_not(here_second)))
        def _():
            out_copy(made, o_send, 0, r, owner, (me + 1) % group).wait_recv()

        return carry

    lax.fori_loop(0, group * per, out_done, 0)


def on_device(queries, keys_values, random_blocks, global_blocks):
    outer, hi, lo = (lax.axis_size(a) for a in ("outer", "hi", "lo"))
    group = outer * lo
    tokens, width = queries.shape
    heads = width // HD // group
    per = tokens // BLOCK
    blocks = group * per
    moved = keys_values.reshape(per, BLOCK, 2, KVH, HD).transpose(3, 0, 2, 1, 4)
    limit = 2 * (hi * blocks * 4 * BLOCK * HD + 3 * tokens * width) + (12 << 20)
    dma = pltpu.SemaphoreType.DMA
    return pl.pallas_call(
        functools.partial(
            fused, outer, hi, lo, per, heads, global_blocks.shape[0], random_blocks.shape[1]
        ),
        in_specs=[pl.BlockSpec(memory_space=pltpu.SMEM)] * 2 + [pl.BlockSpec(memory_space=pl.ANY)] * 2,
        out_specs=pl.BlockSpec(memory_space=pl.ANY),
        out_shape=jax.ShapeDtypeStruct((tokens, width), jnp.bfloat16),
        scratch_shapes=[
            pltpu.VMEM((hi * blocks, 2, BLOCK, HD), jnp.bfloat16),
            pltpu.VMEM((group, tokens, heads * HD), jnp.bfloat16),
            pltpu.VMEM((blocks, BLOCK, heads * HD), jnp.bfloat16),
            pltpu.VMEM((hi * blocks, 2, BLOCK, HD), jnp.bfloat16),
            pltpu.VMEM((group, tokens // 2, heads * HD), jnp.bfloat16),
            pltpu.VMEM((blocks // 2, BLOCK, heads * HD), jnp.bfloat16),
            dma((hi * group,)),
            dma((hi * group,)),
            dma((hi * group,)),
            dma((group,)),
            dma((group,)),
            dma((group,)),
            dma((blocks,)),
            dma((blocks,)),
            dma((2 + per + per // 2,)),
            pltpu.SemaphoreType.REGULAR,
            dma((hi * group,)),
            dma((hi * group,)),
            dma,
            dma,
            dma((blocks // 2,)),
        ],
        compiler_params=pltpu.CompilerParams(collective_id=0, has_side_effects=True, vmem_limit_bytes=limit),
        name="attend",
    )(random_blocks, global_blocks, queries, moved)


def solution(mesh):
    outer, inner = mesh.shape["outer"], mesh.shape["inner"]
    lo = max(1, KVH // outer)
    fine = Mesh(mesh.devices.reshape(outer, inner // lo, lo), ("outer", "hi", "lo"))
    split = ("outer", "hi", "lo")
    return jax.shard_map(
        on_device,
        mesh=fine,
        in_specs=(P(split, None), P(split, None, None), P(), P()),
        out_specs=P(split, None),
        check_vma=False,
    )
```
